128 devices in a mesh: row: 8 (over x_hi, y), col: 16 (over x_lo, z, core).
Axes of the slice: x: 4 (x_hi: 2, x_lo: 2; x = x_hi * 2 + x_lo), y: 4, z: 4, core: 2. Of those that a mesh axis runs over, the one named last changes fastest.
Arguments:
- flexibility: bfloat16 [2048, 384, 384], P(('row', 'col'))
- coupling: bfloat16 [2048, 384, 512], P(('row', 'col')), may hold values from -0.3125 to 0.3125
- boundary: bfloat16 [2048, 512, 512], P(('row', 'col'))
- masses: float32 [2048, 384], P(('row', 'col')), may hold values from 0.5 to 2
- start_modes: bfloat16 [2048, 64, 384], P(('row', 'col')), may hold values from -6 to 6
- interior_sizes: int32 [2048], P(('row', 'col')), may hold values from 128 to 384, as said below
- interface: int32 [2048, 4], P(('row', 'col')), may hold values from 0 to 255, as said below
- start_block: float32 [32, 32768], P(None, ('row', 'col')), may hold values from -6 to 6
Outputs:
- alpha_first: float32 [32, 32], replicated
- alpha_second: float32 [32, 32], replicated
- next_block: float32 [32, 32768], P(None, ('row', 'col'))
- residual_block: float32 [32, 32768], P(None, ('row', 'col'))
- mass_coupling: float32 [2048, 64, 512], P(('row', 'col'))
The draws below stay inside these ranges and needn't reach their ends.
Inputs may be any that keep to these rules, and one draw needn't show every extreme that they name: `interior_sizes`: every device's shard holds a substructure with exactly 384 interior DOFs. `interface`: block id I stands for assembled DOFs 128 I to 128 I + 127; it lies in piece I // 2 of the assembled order, which belongs to row index (I // 2) // (number of col indices) and col index (I // 2) % (number of col indices) of the mesh. The four blocks of one substructure have four different row indices and four different col indices. For every device and every pair of a row index r and a col index c, exactly 2 of the device's 16 substructures have one block at row index r and one block at col index c. Every piece in which some block of a device's substructures lies holds exactly 2 of that device's blocks, counted over its substructures and their four blocks.
All inputs are finite; a program needn't handle non-finite values.
Results may differ from the reference program's by a relative error of at most 0.0083.
Values may be sent and summed in bfloat16 or wider, within the bound.
A program may use at most 192 MiB of HBM per device.

```python
import math
import jax
import jax.numpy as jnp
from jax import lax

TB = 128
NB = 512
NIMAX = 384
NM = 64
NS = 16
ITERS = 4
BW = 32
SUBS = 2048
NA = 32768
N_ROW = 8
N_COL = 16
DEVICES = 128


def symmetric_draw(key, count, order, low, high):
    key_diag, key_off = jax.random.split(key)
    diagonal = jax.random.uniform(key_diag, (count, order), jnp.float32, low, high)
    noise = jax.random.normal(key_off, (count, order, order), jnp.float32) * (0.5 / math.sqrt(order))
    mirrored = (noise + jnp.swapaxes(noise, 1, 2)) * 0.70710678
    identity = jnp.eye(order, dtype=jnp.float32)
    return (mirrored * (1.0 - identity) + diagonal[:, :, None] * identity).astype(jnp.bfloat16)


def draw_flexibility(key, part):
    return symmetric_draw(jax.random.fold_in(key, 11), SUBS, NIMAX, 2.0, 3.0)


def draw_boundary(key, part):
    return symmetric_draw(jax.random.fold_in(key, 23), SUBS, NB, 4.0, 6.0)


def draw_interior_sizes(key, part):
    counts = jax.random.randint(jax.random.fold_in(key, 5), (SUBS,), NIMAX // 3, NIMAX + 1)
    return counts.reshape(DEVICES, NS).at[:, 0].set(NIMAX).reshape(SUBS)


def draw_interface(key, part):
    halves = N_ROW // 4
    quarter = N_COL // 4

    def one_device(device_key):
        key_row, key_col, key_sub, key_bit = jax.random.split(device_key, 4)
        row_order = jax.random.permutation(key_row, N_ROW)
        col_order = jax.random.permutation(key_col, N_COL)
        sub_order = jax.random.permutation(key_sub, NS)
        parity = jax.random.randint(key_bit, (NS, 4), 0, 2)
        members = jnp.arange(NS)[:, None]
        corner = jnp.arange(4)[None, :]
        half_index = members % halves
        group_index = members // halves % quarter
        rows_used = row_order[4 * half_index + corner]
        cols_used = col_order[corner * quarter + group_index]
        block_ids = 2 * (rows_used * N_COL + cols_used) + parity
        return block_ids[sub_order]
    device_keys = jax.random.split(jax.random.fold_in(key, 7), DEVICES)
    return jax.vmap(one_device)(device_keys).reshape(SUBS, 4).astype(jnp.int32)


def block_levels(rng, shape, pieces, smallest, top_value):
    def one(dim, blocks):
        steps = jax.random.uniform(jax.random.fold_in(jax.random.fold_in(rng, 6), dim), (blocks,), jnp.float32, smallest / len(pieces), top_value / len(pieces))
        return jnp.repeat(jnp.exp(steps), shape[dim] // blocks).reshape((-1,) + (1,) * (len(shape) - dim - 1))

    level = one(*pieces[0])
    for cut in pieces[1:]:
        level = level * one(*cut)
    return level


def normal_values(stream_key, shape, deviation, most, cuts=(), kind=jnp.bfloat16):
    gain = block_levels(stream_key, shape, cuts, -0.22, 0.18) if cuts else 1.0
    array = jax.random.normal(stream_key, shape, jnp.float32) * deviation * gain
    return jnp.minimum(jnp.maximum(array, -most), most).astype(kind)


def setup_inputs(seed: int = 0) -> dict:
    seeds = jax.random.split(jax.random.key(seed), 9)
    return {
        "flexibility": draw_flexibility(jax.random.fold_in(seeds[8], 71), 0),
        "coupling": normal_values(seeds[1], (SUBS, NIMAX, NB), NIMAX ** -0.5, 0.3125, ((0, 128),)),
        "boundary": draw_boundary(jax.random.fold_in(seeds[8], 71), 0),
        "masses": jnp.clip(jnp.exp(math.log(2.0) - 1.3862944 * jax.random.uniform(seeds[3], (SUBS, NIMAX), jnp.float32) ** block_levels(seeds[3], (SUBS, NIMAX), ((0, 128),), -0.2, 0.2)), 0.5, 2.0),
        "start_modes": normal_values(seeds[4], (SUBS, NM, NIMAX), 1.0, 6.0, ((0, 128),)),
        "interior_sizes": draw_interior_sizes(jax.random.fold_in(seeds[8], 71), 0),
        "interface": draw_interface(jax.random.fold_in(seeds[8], 71), 0),
        "start_block": normal_values(seeds[7], (BW, NA), 1.0, 6.0, ((1, 128),), jnp.float32),
    }


HIGHEST = lax.Precision.HIGHEST

def condense(flexibility, coupling, boundary, masses, start_modes, interior_count):
    interior = flexibility.shape[0]
    active = (jnp.arange(interior) < interior_count).astype(jnp.float32)
    weight = masses * active
    modes_now = start_modes.astype(jnp.float32) * active
    for sweep in range(ITERS):
        scaled = (modes_now * weight).astype(jnp.bfloat16)
        applied = jnp.dot(scaled.astype(jnp.float32), flexibility.astype(jnp.float32), preferred_element_type=jnp.float32) * active
        gram_matrix = jnp.dot(applied * weight, applied.T, precision=HIGHEST)
        factor = jnp.linalg.cholesky(gram_matrix)
        modes_now = jax.scipy.linalg.solve_triangular(factor, applied, lower=True)
    masked = coupling * active.astype(jnp.bfloat16)[:, None]
    flexed = (jnp.dot(masked.T.astype(jnp.float32), flexibility.astype(jnp.float32), preferred_element_type=jnp.float32) * active).astype(jnp.bfloat16)
    projected = (modes_now * weight).astype(jnp.bfloat16)
    coupling_modal = jnp.dot(projected.astype(jnp.float32), flexed.T.astype(jnp.float32), preferred_element_type=jnp.float32)
    condensed = boundary.astype(jnp.float32) - jnp.dot(flexed.astype(jnp.float32), masked.astype(jnp.float32), preferred_element_type=jnp.float32)
    return (((condensed + condensed.T) * 0.5).astype(jnp.bfloat16), -coupling_modal)

def reference(flexibility, coupling, boundary, masses, start_modes, interior_sizes, interface, start_block):
    tiles, mass_coupling = lax.map(lambda items: condense(*items), (flexibility, coupling, boundary, masses, start_modes, interior_sizes))
    blocks = tiles.reshape(SUBS, 4, TB, 4, TB).transpose(0, 1, 3, 2, 4)

    def apply_matrix(vectors):
        split_vectors = vectors.reshape(BW, NA // TB, TB)

        def add_one(summed, element):
            tile_set, block_ids = element
            gathered = split_vectors[:, block_ids, :]
            product_terms = jnp.einsum('xat,abtu->xbu', gathered, tile_set.astype(jnp.float32), precision=HIGHEST)
            return (summed.at[:, block_ids, :].add(product_terms), None)
        summed, unused = lax.scan(add_one, jnp.zeros((BW, NA // TB, TB), jnp.float32), (blocks, interface))
        return summed.reshape(BW, NA)
    gram_start = jnp.dot(start_block, start_block.T, precision=HIGHEST)
    first_block = jax.scipy.linalg.solve_triangular(jnp.linalg.cholesky(gram_start), start_block, lower=True)
    applied_first = apply_matrix(first_block)
    alpha_first = jnp.dot(applied_first, first_block.T, precision=HIGHEST)
    remainder = applied_first - jnp.dot(alpha_first, first_block, precision=HIGHEST)
    beta_factor = jnp.linalg.cholesky(jnp.dot(remainder, remainder.T, precision=HIGHEST))
    second_block = jax.scipy.linalg.solve_triangular(beta_factor, remainder, lower=True)
    applied_second = apply_matrix(second_block) - jnp.dot(beta_factor.T, first_block, precision=HIGHEST)
    alpha_second = jnp.dot(applied_second, second_block.T, precision=HIGHEST)
    leftover = applied_second - jnp.dot(alpha_second, second_block, precision=HIGHEST)
    rescale = math.sqrt(NA)
    return (alpha_first, alpha_second, rescale * second_block, rescale * leftover, mass_coupling)
```

```python
import functools
import math

import jax
import jax.numpy as jnp
from jax import lax
from jax.experimental import pallas as pl
from jax.experimental.pallas import tpu as pltpu
from jax.sharding import PartitionSpec as P

ITERS = 4
HIGHEST = lax.Precision.HIGHEST
F32 = jnp.float32
BF16 = jnp.bfloat16


def dot(a, b, ca=1, cb=0, precision=None):
    return lax.dot_general(
        a, b, (((ca,), (cb,)), ((), ())), precision=precision, preferred_element_type=F32
    )


def iota(shape, dim):
    return lax.broadcasted_iota(jnp.int32, shape, dim)


def condense_kernel(size_ref, flex_ref, coup_ref, bound_ref, tile_ref):
    count = size_ref[pl.program_id(0)]
    interior = flex_ref.shape[1]
    masked = jnp.where(iota((interior, 1), 0) < count, coup_ref[0], jnp.zeros((), BF16))
    flexed = dot(masked, flex_ref[0], 0, 0)
    flexed = jnp.where(iota((1, interior), 1) < count, flexed, 0.0).astype(BF16)
    edge = tile_ref.shape[3]
    for a in range(4):
        cols = slice(a * edge, (a + 1) * edge)
        part = bound_ref[0, :, cols].astype(F32) - dot(flexed, masked[:, cols])
        tile_ref[0, a] = part.astype(BF16)


def condense(sizes, flexibility, coupling, boundary):
    subs, interior, order = coupling.shape
    edge = order // 4
    return pl.pallas_call(
        condense_kernel,
        out_shape=jax.ShapeDtypeStruct((subs, 4, order, edge), BF16),
        grid_spec=pltpu.PrefetchScalarGridSpec(
            num_scalar_prefetch=1,
            grid=(subs,),
            in_specs=[
                pl.BlockSpec((1, interior, interior), lambda s, n: (s, 0, 0)),
                pl.BlockSpec((1, interior, order), lambda s, n: (s, 0, 0)),
                pl.BlockSpec((1, order, order), lambda s, n: (s, 0, 0)),
            ],
            out_specs=pl.BlockSpec((1, 4, order, edge), lambda s, n: (s, 0, 0, 0)),
        ),
        name="condense",
    )(sizes, flexibility, coupling, boundary)


def lane_pick(x, k):
    return jnp.take_along_axis(x, jnp.full(x.shape, k, jnp.int32), axis=1)


def eliminate(work, subs, order):
    for k in range(order - 1):
        row = work[k]
        scaled_row = row / row[:, k : k + 1]
        tail = work[k + 1 :]
        work[k + 1 :] = tail - tail[:, :, k : k + 1] * scaled_row[None]


def subspace_kernel(
    size_ref, flex_ref, coup_ref, mass_ref, start_ref, out_ref, scaled, applied, work
):
    subs, modes, interior = start_ref.shape
    lanes = iota((1, interior), 1)
    eye = (iota((modes, modes), 0) == iota((modes, modes), 1)).astype(F32)
    diagonal = iota((modes, 128), 0) == iota((modes, 128), 1)

    def weight_of(s):
        return jnp.where(lanes < size_ref[s], mass_ref[s], 0.0)

    for s in range(subs):
        scaled[s] = (start_ref[s].astype(F32) * weight_of(s)).astype(BF16)

    def sweep(i, carry):
        for s in range(subs):
            y = jnp.where(lanes < size_ref[s], dot(scaled[s], flex_ref[s]), 0.0)
            applied[s] = y
            gram = dot(y * weight_of(s), y, 1, 1, HIGHEST)
            work[:, s] = jnp.concatenate([gram, eye], axis=1)
        eliminate(work, subs, modes)
        for s in range(subs):
            done = work[:, s]
            pivots = jnp.sum(jnp.where(diagonal, done, 0.0), axis=1, keepdims=True)
            inverse = done[:, modes:] * lax.rsqrt(pivots)
            x = dot(inverse, applied[s], 1, 0, HIGHEST)
            scaled[s] = (x * weight_of(s)).astype(BF16)
        return carry

    lax.fori_loop(0, ITERS, sweep, 0)

    for s in range(subs):
        v = jnp.where(lanes < size_ref[s], dot(scaled[s], flex_ref[s]), 0.0)
        high = v.astype(BF16)
        low = (v - high.astype(F32)).astype(BF16)
        coupled = coup_ref[s]
        out_ref[s] = -(dot(high, coupled) + dot(low, coupled))


def subspace(sizes, flexibility, coupling, masses, start_modes):
    subs, modes, interior = start_modes.shape
    order = coupling.shape[2]
    vmem = pl.BlockSpec(memory_space=pltpu.VMEM)
    return pl.pallas_call(
        subspace_kernel,
        out_shape=jax.ShapeDtypeStruct((subs, modes, order), F32),
        in_specs=[pl.BlockSpec(memory_space=pltpu.SMEM)] + [vmem] * 4,
        out_specs=vmem,
        scratch_shapes=[
            pltpu.VMEM((subs, modes, interior), BF16),
            pltpu.VMEM((subs, modes, interior), F32),
            pltpu.VMEM((modes, subs, 2 * modes), F32),
        ],
        compiler_params=pltpu.CompilerParams(vmem_limit_bytes=40 * 1024 * 1024),
        name="subspace",
    )(sizes, flexibility, coupling, masses.reshape(subs, 1, interior), start_modes)


def copy_to(axis, peer, src, dst, send, recv):
    return pltpu.make_async_remote_copy(
        src_ref=src,
        dst_ref=dst,
        send_sem=send,
        recv_sem=recv,
        device_id={axis: peer},
        device_id_type=pl.DeviceIdType.MESH,
    )


class Exchange:
    def __init__(self, axis, count, src, dst, per, sems, same=False):
        self.axis, self.count, self.src, self.dst, self.per = axis, count, src, dst, per
        self.send, self.recv, self.same = sems[0], sems[1], same
        self.me = lax.axis_index(axis)

    def part(self, ref, i):
        return ref.at[pl.ds(i * self.per, self.per)]

    def source(self, i):
        return self.src if self.same else self.part(self.src, i)

    def peer(self, i):
        return lax.rem(self.me + i, self.count)

    def start_one(self, peer):
        copy_to(
            self.axis, peer, self.source(peer), self.part(self.dst, self.me),
            self.send.at[peer], self.recv.at[self.me],
        ).start()

    def start(self):
        def body(i, c):
            self.start_one(self.peer(i))
            return c

        lax.fori_loop(1, self.count, body, 0)
        self.keep()

    def keep(self):
        mine = pl.ds(self.me * self.per, self.per)
        self.dst[mine] = self.src[...] if self.same else self.src[mine]

    def wait(self):
        def body(i, c):
            peer = self.peer(i)
            copy = copy_to(
                self.axis, peer, self.source(peer), self.part(self.dst, peer),
                self.send.at[peer], self.recv.at[peer],
            )
            copy.wait_send()
            copy.wait_recv()
            return c

        lax.fori_loop(1, self.count, body, 0)


def small_factor(work, gram):
    order = gram.shape[0]
    eye = (iota((order, order), 0) == iota((order, order), 1)).astype(F32)
    work[:, :order] = gram
    work[:, order : 2 * order] = eye
    work[:, 2 * order :] = jnp.zeros((order, 128 - 2 * order), F32)
    rows = iota((order, 128), 0)

    def body(k, carry):
        row = work[pl.ds(k, 1), :]
        pivot = lane_pick(jnp.broadcast_to(row, (8, 128)), k)[:1]
        full = work[...]
        column = jnp.where(rows > k, lane_pick(full, k), 0.0)
        work[...] = full - column * (row / pivot)
        return carry

    lax.fori_loop(0, order, body, 0)
    done = work[...]
    diagonal = rows == iota((order, 128), 1)
    pivots = jnp.sum(jnp.where(diagonal, done, 0.0), axis=1, keepdims=True)
    done = done * lax.rsqrt(pivots)
    return done[:, :order], done[:, order : 2 * order]


def lanczos_kernel(
    rescale, rows, cols,
    loc_ref, inv_sub_ref, inv_blk_ref, want_ref, start_ref, tile_ref,
    alpha1_ref, alpha2_ref, next_ref, resid_ref,
    xloc, got, pick, have, xs, out, came, part, sums, wants, pay, prow, pcol, work,
    want_smem, tiles, local_sem, tile_sem, *sems,
):
    subs = tile_ref.shape[0]
    width = start_ref.shape[0]
    edge = start_ref.shape[1] // 2
    my_row, my_col = lax.axis_index("row"), lax.axis_index("col")

    barrier = pltpu.get_barrier_semaphore()

    def greet(axis, me, count):
        def body(i, c):
            pl.semaphore_signal(
                barrier, inc=1, device_id={axis: lax.rem(me + i, count)},
                device_id_type=pl.DeviceIdType.MESH,
            )
            return c

        lax.fori_loop(1, count, body, 0)

    greet("row", my_row, rows)
    greet("col", my_col, cols)

    load = pltpu.make_async_copy(tile_ref, tiles, tile_sem)
    load.start()
    pl.semaphore_wait(barrier, rows + cols - 2)

    sems = list(sems)
    ask = Exchange("col", cols, want_ref, wants, 1, sems[0:2])
    ask.start()

    def psum(i, base):
        by_row = Exchange("row", rows, pay.at[i, 0], prow.at[i], 1, sems[base : base + 2], True)
        by_col = Exchange("col", cols, pay.at[i, 1], pcol.at[i], 1, sems[base + 2 : base + 4], True)

        def middle():
            by_row.wait()
            total = prow[i, 0]
            for r in range(1, rows):
                total = total + prow[i, r]
            pay[i, 1, 0] = total
            by_col.start()

        def end():
            by_col.wait()
            total = pcol[i, 0]
            for c in range(1, cols):
                total = total + pcol[i, c]
            return total

        return by_row.start, middle, end

    def spread(i, base):
        first = Exchange("row", rows, xloc.at[i], got.at[i], 2, sems[base : base + 2], True)
        second = Exchange("col", cols, pick.at[i], have.at[i], 4, sems[base + 2 : base + 4])

        def middle():
            first.wait()

            def choose(d, c):
                for k in range(4):
                    pick[i, 4 * d + k] = got[i, want_smem[d, k, 0]]
                return c

            lax.fori_loop(0, cols, choose, 0)
            second.start()

        def end():
            second.wait()

            def gather(s, c):
                for a in range(4):
                    xs[i, s, :, a * edge : (a + 1) * edge] = have[i, loc_ref[4 * s + a]]
                return c

            lax.fori_loop(0, subs, gather, 0)

        return first.start, middle, end

    def multiply(i, base):
        first = Exchange("col", cols, out.at[i], came.at[i], 4, sems[base : base + 2])
        second = Exchange("row", rows, part.at[i], sums.at[i], 2, sems[base + 2 : base + 4])

        def begin():
            def terms(j, c):
                d = lax.rem(my_col + 1 + j, cols)
                for k in range(4):
                    q = 4 * d + k
                    s, a = inv_sub_ref[q], inv_blk_ref[q]
                    out[i, q] = dot(xs[i, s], tiles[s, a]).astype(BF16)

                @pl.when(j < cols - 1)
                def _():
                    first.start_one(d)

                return c

            lax.fori_loop(0, cols, terms, 0)
            first.keep()

        def middle():
            first.wait()
            for h in range(width // 16):
                piece = slice(16 * h, 16 * h + 16)

                def add(c, totals):
                    totals = list(totals)
                    for k in range(4):
                        term = came[i, 4 * c + k, piece].astype(F32)
                        slot = wants[c, k : k + 1, :]
                        for t in range(2 * rows):
                            totals[t] = totals[t] + jnp.where(slot == t, term, 0.0)
                    return tuple(totals)

                zero = jnp.zeros((16, edge), F32)
                totals = lax.fori_loop(0, cols, add, (zero,) * (2 * rows))
                for t in range(2 * rows):
                    part[i, t, piece] = totals[t]
            second.start()

        def end():
            second.wait()
            halves = []
            for p in range(2):
                total = sums[i, p]
                for r in range(1, rows):
                    total = total + sums[i, 2 * r + p]
                halves.append(total)
            return jnp.concatenate(halves, axis=1)

        return begin, middle, end

    def put_vector(i, vector):
        for p in range(2):
            xloc[i, p] = vector[:, p * edge : (p + 1) * edge].astype(BF16)
        return jnp.concatenate([xloc[i, p].astype(F32) for p in range(2)], axis=1)

    zero_pad = jnp.zeros((width, 128 - width), F32)
    start = start_ref[...]
    rounded = put_vector(0, start)
    spread0, sum0 = spread(0, 2), psum(0, 6)
    spread0[0]()
    pay[0, 0, 0] = jnp.concatenate([dot(start, start, 1, 1, HIGHEST), zero_pad], axis=1)
    sum0[0]()
    ask.wait()
    fetch = pltpu.make_async_copy(wants, want_smem, local_sem)
    fetch.start()
    fetch.wait()
    spread0[1]()
    sum0[1]()
    gram = sum0[2]()[:, :width]
    _, inverse0 = small_factor(work, gram)
    q0 = dot(inverse0, rounded, 1, 0, HIGHEST)
    spread0[2]()
    load.wait()

    apply0 = multiply(0, 10)
    apply0[0]()
    apply0[1]()
    w0 = dot(inverse0, apply0[2](), 1, 0, HIGHEST)

    sum1 = psum(1, 14)
    pay[1, 0, 0] = jnp.concatenate(
        [
            dot(w0, q0, 1, 1, HIGHEST),
            dot(w0, w0, 1, 1, HIGHEST),
            dot(q0, q0, 1, 1, HIGHEST),
            jnp.zeros((width, 128 - 3 * width), F32),
        ],
        axis=1,
    )
    sum1[0]()
    sum1[1]()
    total = sum1[2]()
    alpha = total[:, :width]
    alpha1_ref[...] = alpha
    carried = dot(alpha, total[:, 2 * width : 3 * width], 1, 0, HIGHEST) - 2.0 * alpha
    rest = total[:, width : 2 * width] + dot(carried, alpha, 1, 1, HIGHEST)
    beta_t, inverse1 = small_factor(work, rest)
    q1 = dot(inverse1, w0 - dot(alpha, q0, 1, 0, HIGHEST), 1, 0, HIGHEST)
    next_ref[...] = rescale * q1
    rounded1 = put_vector(1, q1)

    spread1 = spread(1, 18)
    spread1[0]()
    back = dot(beta_t, q0, 1, 0, HIGHEST)
    spread1[1]()
    spread1[2]()
    apply1 = multiply(1, 22)
    apply1[0]()
    apply1[1]()
    w1 = apply1[2]() - back

    sum2 = psum(2, 26)
    pay[2, 0, 0] = jnp.concatenate([dot(w1, rounded1, 1, 1, HIGHEST), zero_pad], axis=1)
    sum2[0]()
    sum2[1]()
    alpha2 = sum2[2]()[:, :width]
    alpha2_ref[...] = alpha2
    resid_ref[...] = rescale * (w1 - dot(alpha2, rounded1, 1, 0, HIGHEST))


def routes(interface, rows, cols):
    ids = interface.reshape(-1)
    count = ids.shape[0]
    col = (ids // 2) % cols
    order = jnp.arange(count)
    same = (col[None, :] == col[:, None]) & (order[None, :] < order[:, None])
    loc = col * 4 + jnp.sum(same.astype(jnp.int32), axis=1)
    hit = (loc[None, :] == order[:, None]).astype(jnp.int32)
    inv = jnp.sum(hit * order[None, :], axis=1)
    slot = (ids // 2 // cols) * 2 + ids % 2
    want = jnp.sum(hit * slot[None, :], axis=1).reshape(cols, 4)
    want = jnp.broadcast_to(jnp.pad(want, ((0, 0), (0, 4)))[:, :, None], (cols, 8, 128))
    return loc, inv // 4, inv % 4, want


def lanczos(tiles, interface, start_block, rows, cols):
    subs, _, order, edge = tiles.shape
    width = start_block.shape[0]
    loc, inv_sub, inv_blk, want = routes(interface, rows, cols)
    rescale = math.sqrt(rows * cols * start_block.shape[1])
    vmem = pl.BlockSpec(memory_space=pltpu.VMEM)
    smem = pl.BlockSpec(memory_space=pltpu.SMEM)
    dma = pltpu.SemaphoreType.DMA
    col_pair, row_pair = [dma((cols,))] * 2, [dma((rows,))] * 2
    sums = row_pair + col_pair
    spreads = row_pair + col_pair
    applies = col_pair + row_pair
    return pl.pallas_call(
        functools.partial(lanczos_kernel, rescale, rows, cols),
        out_shape=(
            jax.ShapeDtypeStruct((width, width), F32),
            jax.ShapeDtypeStruct((width, width), F32),
            jax.ShapeDtypeStruct(start_block.shape, F32),
            jax.ShapeDtypeStruct(start_block.shape, F32),
        ),
        in_specs=[smem, smem, smem, vmem, vmem, pl.BlockSpec(memory_space=pl.ANY)],
        out_specs=[vmem] * 4,
        scratch_shapes=[
            pltpu.VMEM((2, 2, width, edge), BF16),
            pltpu.VMEM((2, 2 * rows, width, edge), BF16),
            pltpu.VMEM((2, 4 * cols, width, edge), BF16),
            pltpu.VMEM((2, 4 * cols, width, edge), BF16),
            pltpu.VMEM((2, subs, width, order), BF16),
            pltpu.VMEM((2, 4 * cols, width, edge), BF16),
            pltpu.VMEM((2, 4 * cols, width, edge), BF16),
            pltpu.VMEM((2, 2 * rows, width, edge), F32),
            pltpu.VMEM((2, 2 * rows, width, edge), F32),
            pltpu.VMEM((cols, 8, 128), jnp.int32),
            pltpu.VMEM((3, 2, 1, width, 128), F32),
            pltpu.VMEM((3, rows, width, 128), F32),
            pltpu.VMEM((3, cols, width, 128), F32),
            pltpu.VMEM((width, 128), F32),
            pltpu.SMEM((cols, 8, 128), jnp.int32),
            pltpu.VMEM(tiles.shape, BF16),
            dma,
            dma,
            *col_pair, *spreads, *sums, *applies, *sums, *spreads, *applies, *sums,
        ],
        compiler_params=pltpu.CompilerParams(
            collective_id=0, has_side_effects=True, vmem_limit_bytes=48 * 1024 * 1024
        ),
        name="lanczos",
    )(loc, inv_sub, inv_blk, want, start_block, tiles)


def on_device(
    flexibility, coupling, boundary, masses, start_modes, interior_sizes, interface, start_block
):
    rows, cols = lax.axis_size("row"), lax.axis_size("col")
    tiles = condense(interior_sizes, flexibility, coupling, boundary)
    alpha_first, alpha_second, next_block, residual_block = lanczos(
        tiles, interface, start_block, rows, cols
    )
    mass_coupling = subspace(interior_sizes, flexibility, coupling, masses, start_modes)
    return alpha_first, alpha_second, next_block, residual_block, mass_coupling


def solution(mesh):
    both = ("row", "col")
    return jax.shard_map(
        on_device,
        mesh=mesh,
        in_specs=(
            P(both, None, None),
            P(both, None, None),
            P(both, None, None),
            P(both, None),
            P(both, None, None),
            P(both),
            P(both, None),
            P(None, both),
        ),
        out_specs=(P(), P(), P(None, both), P(None, both), P(both, None, None)),
        check_vma=False,
    )
```

```python
import functools
import math

import jax
import jax.numpy as jnp
from jax import lax
from jax.experimental import pallas as pl
from jax.experimental.pallas import tpu as pltpu
from jax.sharding import PartitionSpec as P

ITERS = 4
HIGHEST = lax.Precision.HIGHEST
F32 = jnp.float32
BF16 = jnp.bfloat16
FILL = (3, 3, 3, 4, 3, 4, 3)
START = (2, 6, 11)


def dot(a, b, ca=1, cb=0, precision=None):
    return lax.dot_general(
        a, b, (((ca,), (cb,)), ((), ())), precision=precision, preferred_element_type=F32
    )


def iota(shape, dim):
    return lax.broadcasted_iota(jnp.int32, shape, dim)


def condense(s, size_ref, flex, coup, bound, tiles):
    interior, edge = flex.shape[1], tiles.shape[3]
    keep = iota((interior, 1), 0) < size_ref[s]
    masked = jnp.where(keep, coup[s], jnp.zeros((), BF16))
    flexed = jnp.where(keep, dot(flex[s], masked), 0.0).astype(BF16)
    for a in range(0, 4, 2):
        cols = slice(a * edge, (a + 2) * edge)
        part = (bound[s, :, cols].astype(F32) - dot(masked, flexed[:, cols], 0, 0)).astype(BF16)
        tiles[s, a] = part[:, :edge]
        tiles[s, a + 1] = part[:, edge:]
    eye = iota((edge, edge), 0) == iota((edge, edge), 1)
    total = jnp.zeros((1, edge), F32)
    for a in range(4):
        block = tiles[s, a, a * edge : (a + 1) * edge].astype(F32)
        total = total + jnp.sum(jnp.where(eye, block, 0.0), axis=0, keepdims=True)
    return total


def lane_pick(x, k):
    return jnp.take_along_axis(x, jnp.full(x.shape, k, jnp.int32), axis=1)


def split(x):
    high = x.astype(BF16)
    return high, (x - high.astype(F32)).astype(BF16)


def eliminate(work, first, last, order):
    half = iota((8, 128), 1) // order * order
    for k in range(first, last):
        at = half + k
        row = work[8 * k : 8 * k + 8]
        scaled_row = row / jnp.take_along_axis(row, at, axis=1)
        here = iota((8, 128), 1) == at
        scaled_row = jnp.where(here, scaled_row / row, scaled_row)
        for i in range(k + 1, order):
            line = work[8 * i : 8 * i + 8]
            factor = jnp.take_along_axis(line, at, axis=1)
            work[8 * i : 8 * i + 8] = jnp.where(here, 0.0, line) - factor * scaled_row


def weight_of(size_ref, mass_ref, s):
    lanes = iota((1, mass_ref.shape[1]), 1)
    return jnp.where(lanes < size_ref[s], mass_ref[s : s + 1], 0.0)


def active(size_ref, s, x):
    return jnp.where(iota((1, x.shape[1]), 1) < size_ref[s], x, 0.0)


def sub_begin(size_ref, mass_ref, start_ref, scaled):
    for s in range(start_ref.shape[0]):
        start = start_ref[s].astype(F32)
        scaled[s] = (start * weight_of(size_ref, mass_ref, s)).astype(BF16)


def sub_before(j, size_ref, flex_ref, mass_ref, scaled, applied, work):
    grams = []
    for s in (j, j + 8):
        y = active(size_ref, s, dot(scaled[s], flex_ref[s]))
        high, low = split(y)
        modes = y.shape[0]
        applied[s, :modes] = high
        applied[s, modes : 2 * modes] = low
        applied[s, 2 * modes :] = high
        left, left_low = split(y * weight_of(size_ref, mass_ref, s))
        grams.append(
            dot(
                jnp.concatenate([left, left, left_low], axis=1),
                jnp.concatenate([high, low, high], axis=1),
                1,
                1,
            )
        )
    work[pl.ds(j, grams[0].shape[0], stride=8), :] = jnp.concatenate(grams, axis=1)


def sub_after(j, size_ref, mass_ref, scaled, applied, work):
    modes = scaled.shape[1]
    both = work[pl.ds(j, modes, stride=8), :]
    lower, row = iota((modes, modes), 1), iota((modes, modes), 0)
    for h in range(2):
        s = j + 8 * h
        done = both[:, h * modes : (h + 1) * modes]
        pivots = jnp.sum(jnp.where(lower == row, done, 0.0), axis=1, keepdims=True)
        inverse = jnp.where(lower < row, done, jnp.where(lower == row, 1.0, 0.0))
        high, low = split(inverse * lax.rsqrt(pivots))
        x = dot(jnp.concatenate([high, high, low], axis=1), applied[s])
        scaled[s] = (x * weight_of(size_ref, mass_ref, s)).astype(BF16)


def sub_last(s, size_ref, flex_ref, coup_ref, scaled, out_ref):
    modes = scaled.shape[1]
    high, low = split(active(size_ref, s, dot(scaled[s], flex_ref[s])))
    both = dot(jnp.concatenate([high, low], axis=0), coup_ref[s])
    out_ref[s] = -(both[:modes] + both[modes:])


def copy_to(axis, peer, src, dst, send, recv):
    return pltpu.make_async_remote_copy(
        src_ref=src,
        dst_ref=dst,
        send_sem=send,
        recv_sem=recv,
        device_id={axis: peer},
        device_id_type=pl.DeviceIdType.MESH,
    )


class Exchange:
    def __init__(self, axis, count, src, dst, per, sems, same=False):
        self.axis, self.count, self.src, self.dst, self.per = axis, count, src, dst, per
        self.send, self.recv, self.same = sems[0], sems[1], same
        self.me = lax.axis_index(axis)

    def part(self, ref, i):
        return ref.at[pl.ds(i * self.per, self.per)]

    def source(self, i):
        return self.src if self.same else self.part(self.src, i)

    def peer(self, i):
        return lax.rem(self.me + i, self.count)

    def start_one(self, peer):
        copy_to(
            self.axis, peer, self.source(peer), self.part(self.dst, self.me),
            self.send.at[peer], self.recv.at[self.me],
        ).start()

    def start(self):
        def body(i, c):
            self.start_one(self.peer(i))
            return c

        lax.fori_loop(1, self.count, body, 0)
        self.keep()

    def keep(self):
        mine = pl.ds(self.me * self.per, self.per)
        self.dst[mine] = self.src[...] if self.same else self.src[mine]

    def described(self, peer):
        return copy_to(
            self.axis, peer, self.source(peer), self.part(self.dst, peer),
            self.send.at[peer], self.recv.at[peer],
        )

    def wait_recv(self, peer):
        self.described(peer).wait_recv()

    def wait_sends(self):
        def body(i, c):
            self.described(self.peer(i)).wait_send()
            return c

        lax.fori_loop(1, self.count, body, 0)

    def wait(self):
        def body(i, c):
            self.wait_recv(self.peer(i))
            return c

        lax.fori_loop(1, self.count, body, 0)
        self.wait_sends()


def small_factor(gram):
    order = gram.shape[0]
    rows, lanes = iota((order, 128), 0), iota((order, 128), 1)
    eye = (iota((order, order), 0) == iota((order, order), 1)).astype(F32)
    x = jnp.concatenate([gram, eye, jnp.zeros((order, 128 - 2 * order), F32)], axis=1)
    for k in range(order - 1):
        row = x[k : k + 1]
        column = jnp.where(rows > k, x[:, k : k + 1], 0.0)
        x = x - column * (row / row[:, k : k + 1])
    pivots = jnp.sum(jnp.where(rows == lanes, x, 0.0), axis=1, keepdims=True)
    x = x * lax.rsqrt(pivots)
    return x[:, :order], x[:, order : 2 * order]


def whole_kernel(
    rescale, rows, cols,
    size_ref, loc_ref, inv_sub_ref, inv_blk_ref, want_ref, start_ref, mass_ref, modes_ref,
    flex_ref, coup_ref, bound_ref,
    small_ref, mass_out_ref,
    xloc, got, pick, have, xs, out, came, part, sums, ask_rows, wants,
    pay, prow, pcol, pay_s, prow_s, pcol_s,
    want_smem, tiles, flex, coup, bound, scaled, applied, work,
    local_sem, load_sem, *sems,
):
    subs, order = bound_ref.shape[:2]
    width = start_ref.shape[0]
    modes = modes_ref.shape[1]
    edge = start_ref.shape[1] // 2
    my_row, my_col = lax.axis_index("row"), lax.axis_index("col")

    barrier = pltpu.get_barrier_semaphore()

    def greet(axis, me, count):
        def body(i, c):
            pl.semaphore_signal(
                barrier, inc=1, device_id={axis: lax.rem(me + i, count)},
                device_id_type=pl.DeviceIdType.MESH,
            )
            return c

        lax.fori_loop(1, count, body, 0)

    greet("row", my_row, rows)
    greet("col", my_col, cols)

    def loads(s):
        pairs = ((flex_ref, flex), (coup_ref, coup), (bound_ref, bound))
        return [
            pltpu.make_async_copy(far.at[s], near.at[s], load_sem.at[n, s])
            for n, (far, near) in enumerate(pairs)
        ]

    def load_all(s, c):
        for load in loads(s):
            load.start()
        return c

    lax.fori_loop(0, subs, load_all, 0)

    def condense_some(first, last):
        def body(s, c):
            for load in loads(s):
                load.wait()
            return c + condense(s, size_ref, flex, coup, bound, tiles)

        return lax.fori_loop(first, last, body, jnp.zeros((1, edge), F32))

    def pieces():
        for _ in range(ITERS):
            for j in range(8):
                sub_before(j, size_ref, flex, mass_ref, scaled, applied, work)
            yield
            for cut in range(0, modes, modes // 4):
                eliminate(work, cut, min(cut + modes // 4, modes - 1), modes)
                yield
            for j in range(8):
                sub_after(j, size_ref, mass_ref, scaled, applied, work)
            yield
        for h in range(2):
            for s in range(h * subs // 2, (h + 1) * subs // 2):
                sub_last(s, size_ref, flex, coup, scaled, mass_out_ref)
            yield

    queue = pieces()

    def fill(count):
        for _ in range(count):
            next(queue, None)

    sems = list(sems)
    def fill_wants(d, c):
        for k in range(4):
            ask_rows[d, k : k + 1, :] = jnp.full((1, 128), want_ref[4 * d + k], jnp.int32)
        ask_rows[d, 4:, :] = jnp.zeros((4, 128), jnp.int32)
        return c

    lax.fori_loop(0, cols, fill_wants, 0)
    ask = Exchange("col", cols, ask_rows, wants, 1, sems[0:2])

    def psum(pay, prow, pcol, i, base):
        by_row = Exchange("row", rows, pay.at[i, 0], prow.at[i], 1, sems[base : base + 2], True)
        by_col = Exchange("col", cols, pay.at[i, 1], pcol.at[i], 1, sems[base + 2 : base + 4], True)

        def middle():
            by_row.wait()
            total = prow[i, 0]
            for r in range(1, rows):
                total = total + prow[i, r]
            pay[i, 1, 0] = total
            by_col.start()

        def end():
            by_col.wait()
            total = pcol[i, 0]
            for c in range(1, cols):
                total = total + pcol[i, c]
            return total

        return by_row.start, middle, end

    def spread(i, base):
        first = Exchange("row", rows, xloc.at[i], got.at[i], 2, sems[base : base + 2], True)
        second = Exchange("col", cols, pick.at[i], have.at[i], 4, sems[base + 2 : base + 4])

        def middle():
            first.wait()

            def choose(j, c):
                d = lax.rem(my_col + 1 + j, cols)

                @pl.when(j > 0)
                def _():
                    second.start_one(lax.rem(my_col + j, cols))

                for k in range(4):
                    pick[i, 4 * d + k] = got[i, want_smem[d, k, 0]]
                return c

            lax.fori_loop(0, cols, choose, 0)
            second.keep()

        def end():
            second.wait()

            def gather(s, c):
                for a in range(4):
                    xs[i, s, :, a * edge : (a + 1) * edge] = have[i, loc_ref[4 * s + a]]
                return c

            lax.fori_loop(0, subs, gather, 0)

        return first.start, middle, end

    def multiply(i, base):
        first = Exchange("col", cols, out.at[i], came.at[i], 4, sems[base : base + 2])
        second = Exchange("row", rows, part.at[i], sums.at[i], 2, sems[base + 2 : base + 4])

        def begin():
            def terms(j, c):
                d = lax.rem(my_col + 1 + j, cols)

                @pl.when(j > 0)
                def _():
                    first.start_one(lax.rem(my_col + j, cols))

                for k in range(4):
                    q = 4 * d + k
                    s, a = inv_sub_ref[q], inv_blk_ref[q]
                    out[i, q] = dot(xs[i, s], tiles[s, a]).astype(BF16)
                return c

            lax.fori_loop(0, cols, terms, 0)
            first.keep()

        def add(c, fresh):
            for h in range(width // 16):
                piece = slice(16 * h, 16 * h + 16)
                terms = [came[i, 4 * c + k, piece].astype(F32) for k in range(4)]
                slots = [wants[c, k : k + 1, :] for k in range(4)]
                for t in range(2 * rows):
                    total = jnp.zeros((16, edge), F32) if fresh else part[i, t, piece]
                    for k in range(4):
                        total = total + jnp.where(slots[k] == t, terms[k], 0.0)
                    part[i, t, piece] = total

        def middle():
            add(my_col, True)

            def take(j, c):
                first.wait_recv(lax.rem(my_col + cols - j, cols))
                add(lax.rem(my_col + cols - j, cols), False)
                return c

            lax.fori_loop(1, cols, take, 0)
            second.start()
            first.wait_sends()

        def end():
            second.wait()
            halves = []
            for p in range(2):
                total = sums[i, p]
                for r in range(1, rows):
                    total = total + sums[i, 2 * r + p]
                halves.append(total)
            return jnp.concatenate(halves, axis=1)

        return begin, middle, end

    def put_vector(i, vector):
        for p in range(2):
            xloc[i, p] = vector[:, p * edge : (p + 1) * edge].astype(BF16)
        return jnp.concatenate([xloc[i, p].astype(F32) for p in range(2)], axis=1)

    def fold(x):
        return jnp.concatenate([x[8 * g : 8 * g + 8] for g in range(width // 8)], axis=1)

    def unfold(x):
        return jnp.concatenate(
            [x[:, width * g : width * g + width] for g in range(width // 8)], axis=0
        )

    def high(a, b, ca=1, cb=0):
        return dot(a, b, ca, cb, HIGHEST)

    pad = jnp.zeros((width, 128 - 2 * width), F32)
    start = start_ref[...]
    rounded = put_vector(0, start)
    spread0, sum0 = spread(0, 2), psum(pay, prow, pcol, 0, 6)
    grams = [high(start, start, 1, 1), high(rounded, rounded, 1, 1), pad]
    pay[0, 0, 0] = jnp.concatenate(grams, axis=1)
    trace = condense_some(0, START[0])
    pl.semaphore_wait(barrier, rows + cols - 2)
    ask.start()
    spread0[0]()
    sum0[0]()
    sub_begin(size_ref, mass_ref, modes_ref, scaled)
    trace = trace + condense_some(START[0], START[1])
    ask.wait()
    fetch = pltpu.make_async_copy(wants, want_smem, local_sem)
    fetch.start()
    fetch.wait()
    spread0[1]()
    sum0[1]()
    trace = trace + condense_some(START[1], START[2])
    grams = sum0[2]()
    _, inverse0 = small_factor(grams[:, :width])
    q0 = high(inverse0, rounded)
    norm0 = high(high(inverse0, grams[:, width : 2 * width]), inverse0, 1, 1)
    trace = trace + condense_some(START[2], subs)
    sum_t = psum(pay_s, prow_s, pcol_s, 0, 14)
    pay_s[0, 0, 0] = jnp.broadcast_to(trace, (8, edge))
    sum_t[0]()
    spread0[2]()

    apply0 = multiply(0, 10)
    apply0[0]()
    fill(FILL[0])
    sum_t[1]()
    apply0[1]()
    fill(FILL[1])
    shift = jnp.sum(sum_t[2]()[:1], axis=1, keepdims=True) / (rows * cols * 2 * edge)
    image = apply0[2]()
    moved = image - shift * rounded
    moved_rounded = put_vector(1, moved)
    spread1 = spread(1, 18)
    spread1[0]()

    v0 = high(inverse0, moved_rounded)
    sum1 = psum(pay, prow, pcol, 1, 22)
    pay[1, 0, 0] = jnp.concatenate([high(v0, q0, 1, 1), high(v0, v0, 1, 1), pad], axis=1)
    sum1[0]()
    w0 = high(inverse0, image)
    v0_full = high(inverse0, moved)
    fill(FILL[2])
    spread1[1]()
    sum1[1]()
    fill(FILL[3])
    spread1[2]()
    apply1 = multiply(1, 26)
    apply1[0]()

    total = sum1[2]()
    cross, square = total[:, :width], total[:, width : 2 * width]
    eye = (iota((width, width), 0) == iota((width, width), 1)).astype(F32)
    alpha = cross + shift * norm0
    less = alpha - shift * eye
    across = high(less, cross, 1, 1)
    rest = square - across - high(cross, less, 1, 1) + high(high(less, norm0), less, 1, 1)
    beta_t, inverse1 = small_factor(rest)
    off = high(less, q0)
    small_ref[:, : 2 * edge] = rescale * high(inverse1, v0_full - off)
    q1 = high(inverse1, v0 - off)
    known = high(inverse1, high(less, w0)) + high(beta_t, q0)
    both_inverse = high(inverse1, inverse0)
    fill(FILL[4])
    apply1[1]()
    fill(FILL[5])
    w1 = high(both_inverse, apply1[2]()) - known

    sum2 = psum(pay_s, prow_s, pcol_s, 1, 30)
    pay_s[1, 0, 0] = fold(high(w1, q1, 1, 1))
    sum2[0]()
    fill(FILL[6])
    sum2[1]()
    fill(100)
    alpha2 = unfold(sum2[2]())
    small_ref[:, 2 * edge : 4 * edge] = rescale * (w1 - high(alpha2, q1))
    small_ref[:, 4 * edge :] = jnp.concatenate([alpha, alpha2, pad], axis=1)


def finish_kernel(
    small_ref, mass_ref, alpha1_ref, alpha2_ref, next_ref, resid_ref, mass_out_ref
):
    width, length = next_ref.shape
    mass_out_ref[...] = mass_ref[...]
    next_ref[...] = small_ref[:, :length]
    resid_ref[...] = small_ref[:, length : 2 * length]
    alpha1_ref[...] = small_ref[:, 2 * length : 2 * length + width]
    alpha2_ref[...] = small_ref[:, 2 * length + width : 2 * length + 2 * width]


def routes(interface, rows, cols):
    ids = interface.reshape(-1)
    count = ids.shape[0]
    col = (ids // 2) % cols
    order = jnp.arange(count)
    same = (col[None, :] == col[:, None]) & (order[None, :] < order[:, None])
    loc = col * 4 + jnp.sum(same.astype(jnp.int32), axis=1)
    hit = (loc[None, :] == order[:, None]).astype(jnp.int32)
    inv = jnp.sum(hit * order[None, :], axis=1)
    slot = (ids // 2 // cols) * 2 + ids % 2
    want = jnp.sum(hit * slot[None, :], axis=1)
    return loc, inv // 4, inv % 4, want


def on_device(
    flexibility, coupling, boundary, masses, start_modes, interior_sizes, interface, start_block
):
    rows, cols = lax.axis_size("row"), lax.axis_size("col")
    subs, interior, order = coupling.shape
    modes = start_modes.shape[1]
    width = start_block.shape[0]
    edge = order // 4
    loc, inv_sub, inv_blk, want = routes(interface, rows, cols)
    rescale = math.sqrt(rows * cols * start_block.shape[1])
    vmem = pl.BlockSpec(memory_space=pltpu.VMEM)
    smem = pl.BlockSpec(memory_space=pltpu.SMEM)
    far = pl.BlockSpec(memory_space=pl.ANY)
    dma = pltpu.SemaphoreType.DMA
    col_pair, row_pair = [dma((cols,))] * 2, [dma((rows,))] * 2
    sums = row_pair + col_pair
    spreads = row_pair + col_pair
    applies = col_pair + row_pair
    small, mass_coupling = pl.pallas_call(
        functools.partial(whole_kernel, rescale, rows, cols),
        out_shape=(
            jax.ShapeDtypeStruct((width, 5 * edge), F32),
            jax.ShapeDtypeStruct((subs, modes, order), F32),
        ),
        in_specs=[smem] * 5 + [vmem] * 3 + [far] * 3,
        out_specs=[vmem] * 2,
        scratch_shapes=[
            pltpu.VMEM((2, 2, width, edge), BF16),
            pltpu.VMEM((2, 2 * rows, width, edge), BF16),
            pltpu.VMEM((2, 4 * cols, width, edge), BF16),
            pltpu.VMEM((2, 4 * cols, width, edge), BF16),
            pltpu.VMEM((2, subs, width, order), BF16),
            pltpu.VMEM((2, 4 * cols, width, edge), BF16),
            pltpu.VMEM((2, 4 * cols, width, edge), BF16),
            pltpu.VMEM((2, 2 * rows, width, edge), F32),
            pltpu.VMEM((2, 2 * rows, width, edge), F32),
            pltpu.VMEM((cols, 8, 128), jnp.int32),
            pltpu.VMEM((cols, 8, 128), jnp.int32),
            pltpu.VMEM((2, 2, 1, width, 128), F32),
            pltpu.VMEM((2, rows, width, 128), F32),
            pltpu.VMEM((2, cols, width, 128), F32),
            pltpu.VMEM((2, 2, 1, 8, 128), F32),
            pltpu.VMEM((2, rows, 8, 128), F32),
            pltpu.VMEM((2, cols, 8, 128), F32),
            pltpu.SMEM((cols, 8, 128), jnp.int32),
            pltpu.VMEM((subs, 4, order, edge), BF16),
            pltpu.VMEM(flexibility.shape, BF16),
            pltpu.VMEM(coupling.shape, BF16),
            pltpu.VMEM(boundary.shape, BF16),
            pltpu.VMEM((subs, modes, interior), BF16),
            pltpu.VMEM((subs, 3 * modes, interior), BF16),
            pltpu.VMEM((8 * modes, 2 * modes), F32),
            dma,
            dma((3, subs)),
            *col_pair, *spreads, *sums, *applies, *sums, *spreads, *sums, *applies, *sums,
        ],
        compiler_params=pltpu.CompilerParams(
            collective_id=0, has_side_effects=True, vmem_limit_bytes=56 * 1024 * 1024
        ),
        name="whole",
    )(
        interior_sizes, loc, inv_sub, inv_blk, want, start_block,
        masses, start_modes, flexibility, coupling, boundary,
    )
    steps = 4
    once = lambda shape: pl.BlockSpec(shape, lambda g: (0, 0))
    slab = pl.BlockSpec((subs // steps, modes, order), lambda g: (g, 0, 0))
    return pl.pallas_call(
        finish_kernel,
        grid=(steps,),
        out_shape=(
            jax.ShapeDtypeStruct((width, width), F32),
            jax.ShapeDtypeStruct((width, width), F32),
            jax.ShapeDtypeStruct(start_block.shape, F32),
            jax.ShapeDtypeStruct(start_block.shape, F32),
            jax.ShapeDtypeStruct((subs, modes, order), F32),
        ),
        in_specs=[once(small.shape), slab],
        out_specs=[once((width, width))] * 2 + [once(start_block.shape)] * 2 + [slab],
        name="finish",
    )(small, mass_coupling)


def solution(mesh):
    both = ("row", "col")
    return jax.shard_map(
        on_device,
        mesh=mesh,
        in_specs=(
            P(both, None, None),
            P(both, None, None),
            P(both, None, None),
            P(both, None),
            P(both, None, None),
            P(both),
            P(both, None),
            P(None, both),
        ),
        out_specs=(P(), P(), P(None, both), P(None, both), P(both, None, None)),
        check_vma=False,
    )
```

```python
import functools
import math

import jax
import jax.numpy as jnp
from jax import lax
from jax.experimental import pallas as pl
from jax.experimental.pallas import tpu as pltpu
from jax.sharding import PartitionSpec as P

ITERS = 4
HIGHEST = lax.Precision.HIGHEST
F32 = jnp.float32
BF16 = jnp.bfloat16
FILL = (3, 3, 3, 4, 1, 3, 2)
START = (2, 6, 11)


def dot(a, b, ca=1, cb=0, precision=None):
    return lax.dot_general(
        a, b, (((ca,), (cb,)), ((), ())), precision=precision, preferred_element_type=F32
    )


def iota(shape, dim):
    return lax.broadcasted_iota(jnp.int32, shape, dim)


def condense(s, size_ref, flex, coup, bound, tiles):
    interior, edge = flex.shape[1], tiles.shape[3]
    keep = iota((interior, 1), 0) < size_ref[s]
    masked = jnp.where(keep, coup[s], jnp.zeros((), BF16))
    flexed = jnp.where(keep, dot(flex[s], masked), 0.0).astype(BF16)
    for a in range(0, 4, 2):
        cols = slice(a * edge, (a + 2) * edge)
        part = (bound[s, :, cols].astype(F32) - dot(masked, flexed[:, cols], 0, 0)).astype(BF16)
        tiles[s, a] = part[:, :edge]
        tiles[s, a + 1] = part[:, edge:]
    eye = iota((edge, edge), 0) == iota((edge, edge), 1)
    total = jnp.zeros((1, edge), F32)
    for a in range(4):
        block = tiles[s, a, a * edge : (a + 1) * edge].astype(F32)
        total = total + jnp.sum(jnp.where(eye, block, 0.0), axis=0, keepdims=True)
    return total


def lane_pick(x, k):
    return jnp.take_along_axis(x, jnp.full(x.shape, k, jnp.int32), axis=1)


def split(x):
    high = x.astype(BF16)
    return high, (x - high.astype(F32)).astype(BF16)


PIVOTS = 2


def eliminate(work, first, last, order):
    lanes = iota((8, 128), 1)
    half = lanes // order * order
    for base in range(first, last, PIVOTS):
        span = range(PIVOTS)
        at = [half + base + q for q in span]
        here = [lanes == at[q] for q in span]
        lines = [work[8 * (base + q) : 8 * (base + q) + 8] for q in span]
        entry = [[jnp.take_along_axis(lines[q], at[r], axis=1) for r in span] for q in span]
        scaled_rows = []
        for q in span:
            scale = 1.0 / entry[q][q]
            scaled_row = jnp.where(here[q], scale, lines[q] * scale)
            for r in range(q + 1, PIVOTS):
                entry[q][r] = entry[q][r] * scale
            for p in range(q + 1, PIVOTS):
                factor = entry[p][q]
                lines[p] = jnp.where(here[q], 0.0, lines[p]) - factor * scaled_row
                for r in range(q + 1, PIVOTS):
                    entry[p][r] = entry[p][r] - factor * entry[q][r]
            for r in range(q + 1, PIVOTS):
                scaled_row = jnp.where(here[r], 0.0, scaled_row)
            scaled_rows.append(scaled_row)
        for q in range(1, PIVOTS):
            work[8 * (base + q) : 8 * (base + q) + 8] = lines[q]
        inside = (lanes >= at[0]) & (lanes <= at[PIVOTS - 1])
        for i in range(base + PIVOTS, order):
            line = work[8 * i : 8 * i + 8]
            factors = [jnp.take_along_axis(line, at[q], axis=1) for q in span]
            line = jnp.where(inside, 0.0, line)
            for q in span:
                for p in range(q):
                    factors[q] = factors[q] - factors[p] * entry[p][q]
                line = line - factors[q] * scaled_rows[q]
            work[8 * i : 8 * i + 8] = line


def weight_of(size_ref, mass_ref, s):
    lanes = iota((1, mass_ref.shape[1]), 1)
    return jnp.where(lanes < size_ref[s], mass_ref[s : s + 1], 0.0)


def active(size_ref, s, x):
    return jnp.where(iota((1, x.shape[1]), 1) < size_ref[s], x, 0.0)


def sub_begin(size_ref, mass_ref, start_ref, scaled):
    for s in range(start_ref.shape[0]):
        start = start_ref[s].astype(F32)
        scaled[s] = (start * weight_of(size_ref, mass_ref, s)).astype(BF16)


def sub_before(j, size_ref, flex_ref, mass_ref, scaled, applied, work):
    grams = []
    for s in (j, j + 8):
        y = active(size_ref, s, dot(scaled[s], flex_ref[s]))
        high, low = split(y)
        modes = y.shape[0]
        applied[s, :modes] = high
        applied[s, modes : 2 * modes] = low
        applied[s, 2 * modes :] = high
        left, left_low = split(y * weight_of(size_ref, mass_ref, s))
        grams.append(
            dot(
                jnp.concatenate([left, left, left_low], axis=1),
                jnp.concatenate([high, low, high], axis=1),
                1,
                1,
            )
        )
    work[pl.ds(j, grams[0].shape[0], stride=8), :] = jnp.concatenate(grams, axis=1)


def sub_after(j, size_ref, mass_ref, scaled, applied, work):
    modes = scaled.shape[1]
    both = work[pl.ds(j, modes, stride=8), :]
    lower, row = iota((modes, modes), 1), iota((modes, modes), 0)
    for h in range(2):
        s = j + 8 * h
        done = both[:, h * modes : (h + 1) * modes]
        pivots = jnp.sum(jnp.where(lower == row, done, 0.0), axis=1, keepdims=True)
        inverse = jnp.where(lower < row, done, jnp.where(lower == row, 1.0, 0.0))
        high, low = split(inverse * lax.rsqrt(pivots))
        x = dot(jnp.concatenate([high, high, low], axis=1), applied[s])
        scaled[s] = (x * weight_of(size_ref, mass_ref, s)).astype(BF16)


def sub_last(s, size_ref, flex_ref, coup_ref, scaled, out_ref):
    modes = scaled.shape[1]
    high, low = split(active(size_ref, s, dot(scaled[s], flex_ref[s])))
    both = dot(jnp.concatenate([high, low], axis=0), coup_ref[s])
    out_ref[s] = -(both[:modes] + both[modes:])


def copy_to(axis, peer, src, dst, send, recv):
    return pltpu.make_async_remote_copy(
        src_ref=src,
        dst_ref=dst,
        send_sem=send,
        recv_sem=recv,
        device_id={axis: peer},
        device_id_type=pl.DeviceIdType.MESH,
    )


class Exchange:
    def __init__(self, axis, count, src, dst, per, sems, same=False):
        self.axis, self.count, self.src, self.dst, self.per = axis, count, src, dst, per
        self.send, self.recv, self.same = sems[0], sems[1], same
        self.me = lax.axis_index(axis)

    def part(self, ref, i):
        return ref.at[pl.ds(i * self.per, self.per)]

    def source(self, i):
        return self.src if self.same else self.part(self.src, i)

    def peer(self, i):
        return lax.rem(self.me + i, self.count)

    def start_one(self, peer):
        copy_to(
            self.axis, peer, self.source(peer), self.part(self.dst, self.me),
            self.send.at[peer], self.recv.at[self.me],
        ).start()

    def start(self):
        def body(i, c):
            self.start_one(self.peer(i))
            return c

        lax.fori_loop(1, self.count, body, 0)
        self.keep()

    def keep(self):
        mine = pl.ds(self.me * self.per, self.per)
        self.dst[mine] = self.src[...] if self.same else self.src[mine]

    def described(self, peer):
        return copy_to(
            self.axis, peer, self.source(peer), self.part(self.dst, peer),
            self.send.at[peer], self.recv.at[peer],
        )

    def wait_recv(self, peer):
        self.described(peer).wait_recv()

    def wait_sends(self):
        def body(i, c):
            self.described(self.peer(i)).wait_send()
            return c

        lax.fori_loop(1, self.count, body, 0)

    def wait(self):
        def body(i, c):
            self.wait_recv(self.peer(i))
            return c

        lax.fori_loop(1, self.count, body, 0)
        self.wait_sends()


def small_factor(gram):
    order = gram.shape[0]
    rows, lanes = iota((order, 128), 0), iota((order, 128), 1)
    eye = (iota((order, order), 0) == iota((order, order), 1)).astype(F32)
    x = jnp.concatenate([gram, eye, jnp.zeros((order, 128 - 2 * order), F32)], axis=1)
    for k in range(order - 1):
        row = x[k : k + 1]
        column = jnp.where(rows > k, x[:, k : k + 1], 0.0)
        x = x - column * (row / row[:, k : k + 1])
    pivots = jnp.sum(jnp.where(rows == lanes, x, 0.0), axis=1, keepdims=True)
    x = x * lax.rsqrt(pivots)
    return x[:, :order], x[:, order : 2 * order]


def whole_kernel(
    rescale, rows, cols,
    size_ref, loc_ref, inv_sub_ref, inv_blk_ref, want_ref, start_ref, mass_ref, modes_ref,
    flex_ref, coup_ref, bound_ref,
    small_ref, mass_out_ref,
    xloc, got, pick, have, xs, out, came, part, sums, ask_rows, wants,
    pay, prow, pcol, pay_s, prow_s, pcol_s,
    want_smem, tiles, flex, coup, bound, scaled, applied, work,
    local_sem, load_sem, *sems,
):
    subs, order = bound_ref.shape[:2]
    width = start_ref.shape[0]
    modes = modes_ref.shape[1]
    edge = start_ref.shape[1] // 2
    my_row, my_col = lax.axis_index("row"), lax.axis_index("col")

    barrier = pltpu.get_barrier_semaphore()

    def greet(axis, me, count):
        def body(i, c):
            pl.semaphore_signal(
                barrier, inc=1, device_id={axis: lax.rem(me + i, count)},
                device_id_type=pl.DeviceIdType.MESH,
            )
            return c

        lax.fori_loop(1, count, body, 0)

    greet("row", my_row, rows)
    greet("col", my_col, cols)

    def loads(s):
        pairs = ((flex_ref, flex), (coup_ref, coup), (bound_ref, bound))
        return [
            pltpu.make_async_copy(far.at[s], near.at[s], load_sem.at[n, s])
            for n, (far, near) in enumerate(pairs)
        ]

    def load_all(s, c):
        for load in loads(s):
            load.start()
        return c

    lax.fori_loop(0, subs, load_all, 0)

    def condense_some(first, last):
        def body(s, c):
            for load in loads(s):
                load.wait()
            return c + condense(s, size_ref, flex, coup, bound, tiles)

        return lax.fori_loop(first, last, body, jnp.zeros((1, edge), F32))

    def pieces():
        for _ in range(ITERS):
            for j in range(8):
                sub_before(j, size_ref, flex, mass_ref, scaled, applied, work)
            yield
            for first, last in ((0, 12), (12, 28), (28, modes)):
                eliminate(work, first, last, modes)
                yield
            for j in range(8):
                sub_after(j, size_ref, mass_ref, scaled, applied, work)
            yield
        for h in range(2):
            for s in range(h * subs // 2, (h + 1) * subs // 2):
                sub_last(s, size_ref, flex, coup, scaled, mass_out_ref)
            yield

    queue = pieces()

    def fill(count):
        for _ in range(count):
            next(queue, None)

    sems = list(sems)
    def fill_wants(d, c):
        for k in range(4):
            ask_rows[d, k : k + 1, :] = jnp.full((1, 128), want_ref[4 * d + k], jnp.int32)
        ask_rows[d, 4:, :] = jnp.zeros((4, 128), jnp.int32)
        return c

    lax.fori_loop(0, cols, fill_wants, 0)
    ask = Exchange("col", cols, ask_rows, wants, 1, sems[0:2])

    def psum(pay, prow, pcol, i, base):
        by_row = Exchange("row", rows, pay.at[i, 0], prow.at[i], 1, sems[base : base + 2], True)
        by_col = Exchange("col", cols, pay.at[i, 1], pcol.at[i], 1, sems[base + 2 : base + 4], True)

        def middle():
            by_row.wait()
            total = prow[i, 0]
            for r in range(1, rows):
                total = total + prow[i, r]
            pay[i, 1, 0] = total
            by_col.start()

        def end():
            by_col.wait()
            total = pcol[i, 0]
            for c in range(1, cols):
                total = total + pcol[i, c]
            return total

        return by_row.start, middle, end

    def spread(i, base):
        first = Exchange("row", rows, xloc.at[i], got.at[i], 2, sems[base : base + 2], True)
        second = Exchange("col", cols, pick.at[i], have.at[i], 4, sems[base + 2 : base + 4])

        def middle():
            first.wait()

            def choose(j, c):
                d = lax.rem(my_col + 1 + j, cols)

                @pl.when(j > 0)
                def _():
                    second.start_one(lax.rem(my_col + j, cols))

                for k in range(4):
                    pick[i, 4 * d + k] = got[i, want_smem[d, k, 0]]
                return c

            lax.fori_loop(0, cols, choose, 0)
            second.keep()

        def end():
            second.wait()

            def gather(s, c):
                for a in range(4):
                    xs[i, s, :, a * edge : (a + 1) * edge] = have[i, loc_ref[4 * s + a]]
                return c

            lax.fori_loop(0, subs, gather, 0)

        return first.start, middle, end

    def multiply(i, base):
        first = Exchange("col", cols, out.at[i], came.at[i], 4, sems[base : base + 2])
        second = Exchange("row", rows, part.at[i], sums.at[i], 2, sems[base + 2 : base + 4])

        def begin():
            def terms(j, c):
                d = lax.rem(my_col + 1 + j, cols)

                @pl.when(j > 0)
                def _():
                    first.start_one(lax.rem(my_col + j, cols))

                for k in range(4):
                    q = 4 * d + k
                    s, a = inv_sub_ref[q], inv_blk_ref[q]
                    out[i, q] = dot(xs[i, s], tiles[s, a]).astype(BF16)
                return c

            lax.fori_loop(0, cols, terms, 0)
            first.keep()

        def add(c, fresh):
            for h in range(width // 16):
                piece = slice(16 * h, 16 * h + 16)
                terms = [came[i, 4 * c + k, piece].astype(F32) for k in range(4)]
                slots = [wants[c, k : k + 1, :] for k in range(4)]
                for t in range(2 * rows):
                    total = jnp.zeros((16, edge), F32) if fresh else part[i, t, piece]
                    for k in range(4):
                        total = total + jnp.where(slots[k] == t, terms[k], 0.0)
                    part[i, t, piece] = total

        def middle():
            add(my_col, True)

            def take(j, c):
                first.wait_recv(lax.rem(my_col + cols - j, cols))
                add(lax.rem(my_col + cols - j, cols), False)
                return c

            lax.fori_loop(1, cols, take, 0)
            second.start()
            first.wait_sends()

        def end():
            second.wait()
            halves = []
            for p in range(2):
                total = sums[i, p]
                for r in range(1, rows):
                    total = total + sums[i, 2 * r + p]
                halves.append(total)
            return jnp.concatenate(halves, axis=1)

        return begin, middle, end

    def put_vector(i, vector):
        for p in range(2):
            xloc[i, p] = vector[:, p * edge : (p + 1) * edge].astype(BF16)
        return jnp.concatenate([xloc[i, p].astype(F32) for p in range(2)], axis=1)

    def fold(x):
        return jnp.concatenate([x[8 * g : 8 * g + 8] for g in range(width // 8)], axis=1)

    def unfold(x):
        return jnp.concatenate(
            [x[:, width * g : width * g + width] for g in range(width // 8)], axis=0
        )

    def high(a, b, ca=1, cb=0):
        return dot(a, b, ca, cb, HIGHEST)

    pad = jnp.zeros((width, 128 - 2 * width), F32)
    start = start_ref[...]
    rounded = put_vector(0, start)
    spread0, sum0 = spread(0, 2), psum(pay, prow, pcol, 0, 6)
    grams = [high(start, start, 1, 1), high(rounded, rounded, 1, 1), pad]
    pay[0, 0, 0] = jnp.concatenate(grams, axis=1)
    trace = condense_some(0, START[0])
    pl.semaphore_wait(barrier, rows + cols - 2)
    ask.start()
    spread0[0]()
    sum0[0]()
    sub_begin(size_ref, mass_ref, modes_ref, scaled)
    trace = trace + condense_some(START[0], START[1])
    ask.wait()
    fetch = pltpu.make_async_copy(wants, want_smem, local_sem)
    fetch.start()
    fetch.wait()
    spread0[1]()
    sum0[1]()
    trace = trace + condense_some(START[1], START[2])
    grams = sum0[2]()
    _, inverse0 = small_factor(grams[:, :width])
    q0 = high(inverse0, rounded)
    norm0 = high(high(inverse0, grams[:, width : 2 * width]), inverse0, 1, 1)
    trace = trace + condense_some(START[2], subs)
    sum_t = psum(pay_s, prow_s, pcol_s, 0, 14)
    pay_s[0, 0, 0] = jnp.broadcast_to(trace, (8, edge))
    sum_t[0]()
    spread0[2]()

    apply0 = multiply(0, 10)
    apply0[0]()
    fill(FILL[0])
    sum_t[1]()
    apply0[1]()
    fill(FILL[1])
    shift = jnp.sum(sum_t[2]()[:1], axis=1, keepdims=True) / (rows * cols * 2 * edge)
    image = apply0[2]()
    moved = image - shift * rounded
    moved_rounded = put_vector(1, moved)
    spread1 = spread(1, 18)
    spread1[0]()

    v0 = high(inverse0, moved_rounded)
    sum1 = psum(pay, prow, pcol, 1, 22)
    pay[1, 0, 0] = jnp.concatenate([high(v0, q0, 1, 1), high(v0, v0, 1, 1), pad], axis=1)
    sum1[0]()
    w0 = high(inverse0, image)
    v0_full = high(inverse0, moved)
    fill(FILL[2])
    spread1[1]()
    sum1[1]()
    fill(FILL[3])
    spread1[2]()
    apply1 = multiply(1, 26)
    apply1[0]()

    total = sum1[2]()
    cross, square = total[:, :width], total[:, width : 2 * width]
    eye = (iota((width, width), 0) == iota((width, width), 1)).astype(F32)
    alpha = cross + shift * norm0
    less = alpha - shift * eye
    across = high(less, cross, 1, 1)
    rest = square - across - high(cross, less, 1, 1) + high(high(less, norm0), less, 1, 1)
    beta_t, inverse1 = small_factor(rest)
    off = high(less, q0)
    small_ref[:, : 2 * edge] = rescale * high(inverse1, v0_full - off)
    q1 = high(inverse1, v0 - off)
    known = high(inverse1, high(less, w0)) + high(beta_t, q0)
    both_inverse = high(inverse1, inverse0)
    fill(FILL[4])
    apply1[1]()
    fill(FILL[5])
    w1 = high(both_inverse, apply1[2]()) - known

    sum2 = psum(pay_s, prow_s, pcol_s, 1, 30)
    pay_s[1, 0, 0] = fold(high(w1, q1, 1, 1))
    sum2[0]()
    fill(FILL[6])
    sum2[1]()
    fill(100)
    alpha2 = unfold(sum2[2]())
    small_ref[:, 2 * edge : 4 * edge] = rescale * (w1 - high(alpha2, q1))
    small_ref[:, 4 * edge :] = jnp.concatenate([alpha, alpha2, pad], axis=1)


def finish_kernel(
    small_ref, mass_ref, alpha1_ref, alpha2_ref, next_ref, resid_ref, mass_out_ref
):
    width, length = next_ref.shape
    mass_out_ref[...] = mass_ref[...]
    next_ref[...] = small_ref[:, :length]
    resid_ref[...] = small_ref[:, length : 2 * length]
    alpha1_ref[...] = small_ref[:, 2 * length : 2 * length + width]
    alpha2_ref[...] = small_ref[:, 2 * length + width : 2 * length + 2 * width]


def routes(interface, rows, cols):
    ids = interface.reshape(-1)
    count = ids.shape[0]
    col = (ids // 2) % cols
    order = jnp.arange(count)
    same = (col[None, :] == col[:, None]) & (order[None, :] < order[:, None])
    loc = col * 4 + jnp.sum(same.astype(jnp.int32), axis=1)
    hit = (loc[None, :] == order[:, None]).astype(jnp.int32)
    inv = jnp.sum(hit * order[None, :], axis=1)
    slot = (ids // 2 // cols) * 2 + ids % 2
    want = jnp.sum(hit * slot[None, :], axis=1)
    return loc, inv // 4, inv % 4, want


def on_device(
    flexibility, coupling, boundary, masses, start_modes, interior_sizes, interface, start_block
):
    rows, cols = lax.axis_size("row"), lax.axis_size("col")
    subs, interior, order = coupling.shape
    modes = start_modes.shape[1]
    width = start_block.shape[0]
    edge = order // 4
    loc, inv_sub, inv_blk, want = routes(interface, rows, cols)
    rescale = math.sqrt(rows * cols * start_block.shape[1])
    vmem = pl.BlockSpec(memory_space=pltpu.VMEM)
    smem = pl.BlockSpec(memory_space=pltpu.SMEM)
    far = pl.BlockSpec(memory_space=pl.ANY)
    dma = pltpu.SemaphoreType.DMA
    col_pair, row_pair = [dma((cols,))] * 2, [dma((rows,))] * 2
    sums = row_pair + col_pair
    spreads = row_pair + col_pair
    applies = col_pair + row_pair
    small, mass_coupling = pl.pallas_call(
        functools.partial(whole_kernel, rescale, rows, cols),
        out_shape=(
            jax.ShapeDtypeStruct((width, 5 * edge), F32),
            jax.ShapeDtypeStruct((subs, modes, order), F32),
        ),
        in_specs=[smem] * 5 + [vmem] * 3 + [far] * 3,
        out_specs=[vmem] * 2,
        scratch_shapes=[
            pltpu.VMEM((2, 2, width, edge), BF16),
            pltpu.VMEM((2, 2 * rows, width, edge), BF16),
            pltpu.VMEM((2, 4 * cols, width, edge), BF16),
            pltpu.VMEM((2, 4 * cols, width, edge), BF16),
            pltpu.VMEM((2, subs, width, order), BF16),
            pltpu.VMEM((2, 4 * cols, width, edge), BF16),
            pltpu.VMEM((2, 4 * cols, width, edge), BF16),
            pltpu.VMEM((2, 2 * rows, width, edge), F32),
            pltpu.VMEM((2, 2 * rows, width, edge), F32),
            pltpu.VMEM((cols, 8, 128), jnp.int32),
            pltpu.VMEM((cols, 8, 128), jnp.int32),
            pltpu.VMEM((2, 2, 1, width, 128), F32),
            pltpu.VMEM((2, rows, width, 128), F32),
            pltpu.VMEM((2, cols, width, 128), F32),
            pltpu.VMEM((2, 2, 1, 8, 128), F32),
            pltpu.VMEM((2, rows, 8, 128), F32),
            pltpu.VMEM((2, cols, 8, 128), F32),
            pltpu.SMEM((cols, 8, 128), jnp.int32),
            pltpu.VMEM((subs, 4, order, edge), BF16),
            pltpu.VMEM(flexibility.shape, BF16),
            pltpu.VMEM(coupling.shape, BF16),
            pltpu.VMEM(boundary.shape, BF16),
            pltpu.VMEM((subs, modes, interior), BF16),
            pltpu.VMEM((subs, 3 * modes, interior), BF16),
            pltpu.VMEM((8 * modes, 2 * modes), F32),
            dma,
            dma((3, subs)),
            *col_pair, *spreads, *sums, *applies, *sums, *spreads, *sums, *applies, *sums,
        ],
        compiler_params=pltpu.CompilerParams(
            collective_id=0, has_side_effects=True, vmem_limit_bytes=56 * 1024 * 1024
        ),
        name="whole",
    )(
        interior_sizes, loc, inv_sub, inv_blk, want, start_block,
        masses, start_modes, flexibility, coupling, boundary,
    )
    steps = 4
    once = lambda shape: pl.BlockSpec(shape, lambda g: (0, 0))
    slab = pl.BlockSpec((subs // steps, modes, order), lambda g: (g, 0, 0))
    return pl.pallas_call(
        finish_kernel,
        grid=(steps,),
        out_shape=(
            jax.ShapeDtypeStruct((width, width), F32),
            jax.ShapeDtypeStruct((width, width), F32),
            jax.ShapeDtypeStruct(start_block.shape, F32),
            jax.ShapeDtypeStruct(start_block.shape, F32),
            jax.ShapeDtypeStruct((subs, modes, order), F32),
        ),
        in_specs=[once(small.shape), slab],
        out_specs=[once((width, width))] * 2 + [once(start_block.shape)] * 2 + [slab],
        name="finish",
    )(small, mass_coupling)


def solution(mesh):
    both = ("row", "col")
    return jax.shard_map(
        on_device,
        mesh=mesh,
        in_specs=(
            P(both, None, None),
            P(both, None, None),
            P(both, None, None),
            P(both, None),
            P(both, None, None),
            P(both),
            P(both, None),
            P(None, both),
        ),
        out_specs=(P(), P(), P(None, both), P(None, both), P(both, None, None)),
        check_vma=False,
    )
```
